512 devices in a mesh: row: 64 (over z_hi, x, y), col: 8 (over z_lo, core).
Axes of the slice: x: 4, y: 4, z: 16 (z_hi: 4, z_lo: 4; z = z_hi * 4 + z_lo), core: 2. Of those that a mesh axis runs over, the one named last changes fastest.
Arguments:
- tensor: float32 [8, 8192, 8192], P(None, 'row', 'col'), may hold values from -0.8 to 0.8
- factor_a: float32 [8192, 256], P(('row', 'col')), may hold values from -0.0625 to 0.0625
- factor_bt: float32 [256, 8192], P('row', 'col'), may hold values from -0.0625 to 0.0625
- factor_c: float32 [8, 256], replicated, may hold values from -6 to 6
Outputs:
- grad_a: float32 [8192, 256], P(('row', 'col'))
- grad_bt: float32 [256, 8192], P('row', 'col')
- grad_c: float32 [8, 256], replicated
The draws below stay inside these ranges and needn't reach their ends.
All inputs are finite; a program needn't handle non-finite values.
Results may differ from the reference program's by a relative error of at most 0.0001.
Values sent between devices are 32-bit elements; how exact they have to be, the bound alone decides.
A program may use at most 64 MiB of HBM per device.

```python
import jax
import jax.numpy as jnp
from jax import lax

R = 256
K = 8
I = 8192
J = 8192


def steps_of(rng, shape, shards, low, largest):
    def one(axis_at, parts):
        steps = jax.random.uniform(jax.random.fold_in(jax.random.fold_in(rng, 6), axis_at), (parts,), jnp.float32, low / len(shards), largest / len(shards))
        return jnp.repeat(jnp.exp(steps), shape[axis_at] // parts).reshape((-1,) + (1,) * (len(shape) - axis_at - 1))

    gain = one(*shards[0])
    for cut in shards[1:]:
        gain = gain * one(*cut)
    return gain


def bell_draw(own_key, dims, deviation, bound, pieces=(), held_as=jnp.bfloat16):
    array = deviation * jax.random.normal(own_key, dims, jnp.float32)
    if pieces:
        array = array * steps_of(own_key, dims, pieces, -0.22, 0.18)
    return jnp.clip(array, -bound, bound).astype(held_as)


def setup_inputs(seed: int = 0) -> dict:
    key_list = jax.random.split(jax.random.key(seed), 5)
    tensor = bell_draw(key_list[0], (K, I, J), 0.1, 0.8, ((1, 64), (2, 8)), jnp.float32)
    factor_a = bell_draw(key_list[1], (I, R), I ** -0.5, 0.0625, ((0, 512),), jnp.float32)
    factor_bt = bell_draw(key_list[2], (R, J), J ** -0.5, 0.0625, ((0, 64), (1, 8)), jnp.float32)
    factor_c = bell_draw(key_list[3], (K, R), 1.0, 6.0, (), jnp.float32)
    return {"tensor": tensor, "factor_a": factor_a, "factor_bt": factor_bt, "factor_c": factor_c}


def reference(tensor, factor_a, factor_bt, factor_c):
    highest = lax.Precision.HIGHEST
    gram_a = jnp.dot(factor_a.T, factor_a, precision=highest)
    gram_b = jnp.dot(factor_bt, factor_bt.T, precision=highest)
    gram_c = jnp.dot(factor_c.T, factor_c, precision=highest)

    def slice_step(carry, inputs):
        sum_a, sum_bt = carry
        slab, c_row = inputs
        contracted = jnp.dot(slab, factor_bt.T, precision=highest)
        sum_a = sum_a + c_row[None, :] * contracted
        c_term = jnp.sum(factor_a * contracted, axis=0)
        sum_bt = sum_bt + jnp.dot((factor_a * c_row[None, :]).T, slab, precision=highest)
        return (sum_a, sum_bt), c_term

    start_a = jnp.zeros(factor_a.shape, factor_a.dtype)
    start_bt = jnp.zeros(factor_bt.shape, factor_bt.dtype)
    (mttkrp_a, mttkrp_bt), mttkrp_c = lax.scan(slice_step, (start_a, start_bt), (tensor, factor_c))
    grad_a = jnp.dot(factor_a, gram_b * gram_c, precision=highest) - mttkrp_a
    grad_bt = jnp.dot(gram_a * gram_c, factor_bt, precision=highest) - mttkrp_bt
    grad_c = jnp.dot(factor_c, gram_a * gram_b, precision=highest) - mttkrp_c
    return grad_a, grad_bt, grad_c
```

```python
import jax
import jax.numpy as jnp
from jax import lax
from jax.experimental import pallas as pl
from jax.experimental.pallas import tpu as pltpu
from jax.sharding import PartitionSpec as P

MESH = pl.DeviceIdType.MESH
F32, BF16 = jnp.float32, jnp.bfloat16
NSEM = 160
NN = (((1,), (0,)), ((), ()))
NT = (((1,), (1,)), ((), ()))


def split(v):
    hi = v.astype(BF16)
    return hi, (v - hi.astype(F32)).astype(BF16)


def dot3(a, b, dims):
    def one(u, v):
        return lax.dot_general(u, v, dims, preferred_element_type=F32)

    return one(a[0], b[0]) + (one(a[0], b[1]) + one(a[1], b[0]))


def kernel(
    t_hbm, a_ref, bt_ref, c_ref,
    ga_out, gbt_out, gc_out,
    tf, thi, tlo, whi, wlo, m1, ab, bg, btn, bhi, blo, hm, gam, gcm, gbm,
    gr, r1, r2, z1, z2, pa, pcore, psum, pz, pck, cown, ccore, cx, cy, cz, ch, cf,
    ct, ssem, rsem, lsem,
):
    row, col = lax.axis_index("row"), lax.axis_index("col")
    zh, x, y = row // 16, (row // 4) % 4, row % 4
    zl, core = col // 2, col % 2
    other = 1 - core

    def at_row(h, i, j):
        return (h * 16 + i * 4 + j, col)

    def xp(d):
        return at_row(zh, (x + d) % 4, y)

    def yp(d):
        return at_row(zh, x, (y + d) % 4)

    def zp(d):
        return at_row((zh + d) % 4, x, y)

    def lp(d):
        return (row, ((zl + d) % 4) * 2 + core)

    twin = (row, zl * 2 + other)
    sent = []

    def send(src, dst, device):
        k = len(sent)
        copy = pltpu.make_async_remote_copy(
            src_ref=src, dst_ref=dst, send_sem=ssem.at[k], recv_sem=rsem.at[k],
            device_id=device, device_id_type=MESH,
        )
        copy.start()
        sent.append(copy)
        return copy

    def arrive(copies):
        for copy in copies:
            copy.wait_recv()

    load_t = pltpu.make_async_copy(t_hbm, tf, lsem.at[0])
    load_t.start()
    own_bt = pltpu.make_async_copy(bt_ref, bg.at[zh, x, y], lsem.at[1])
    own_bt.start()
    own_a = pltpu.make_async_copy(a_ref, ab.at[zl, core], lsem.at[2])
    own_a.start()

    barrier = pltpu.get_barrier_semaphore()
    peers = [f(d) for f in (xp, yp, lp) for d in (1, 2, 3)] + [zp(1), zp(3), twin]
    for device in peers:
        pl.semaphore_signal(barrier, inc=1, device_id=device, device_id_type=MESH)
    pl.semaphore_wait(barrier, len(peers))

    def stage1(w, slot):
        return [send(slot.at[0], bg.at[w, x, y, 0], xp(d)) for d in (1, 2, 3)] + [
            send(slot.at[1], bg.at[w, x, y, 1], yp(d)) for d in (1, 2, 3)
        ]

    def stage2(w):
        return [
            send(bg.at[w, :, y, 0], bg.at[w, :, y, 0], yp(d)) for d in (1, 2, 3)
        ] + [send(bg.at[w, x, :, 1], bg.at[w, x, :, 1], xp(d)) for d in (1, 2, 3)]

    up, down, far = (zh + 1) % 4, (zh + 3) % 4, (zh + 2) % 4
    mine = bg.at[zh, x, y]
    z_up = send(bt_ref, mine, zp(1))
    z_down = send(bt_ref, mine, zp(3))
    a_line = [send(a_ref, ab.at[zl, core], lp(d)) for d in (1, 2, 3)]
    own1 = stage1(zh, bt_ref)
    own_bt.wait()
    own_a.wait()

    load_t.wait()

    def split_t(k, _):
        hi, lo = split(tf[k])
        at = pl.ds(pl.multiple_of(k * 128, 128), 128)
        thi[at, :] = hi
        tlo[at, :] = lo
        return 0

    lax.fori_loop(0, 4, split_t, 0)
    arrive(own1)
    own2 = stage2(zh)
    arrive(a_line)
    a_twin = send(ab.at[:, core], ab.at[:, core], twin)
    z_up.wait_recv()
    on_up = send(bg.at[down, x, y, 0], bg.at[down, x, y, 0], zp(1))
    down1 = stage1(down, bg.at[down, x, y])
    z_down.wait_recv()
    on_down = send(bg.at[up, x, y, 1], bg.at[up, x, y, 1], zp(3))
    up1 = stage1(up, bg.at[up, x, y])
    lax.fori_loop(4, 8, split_t, 0)

    a_twin.wait_recv()
    block_a = ab[...].reshape(128, 256)
    c_all = c_ref[...]
    a_t = jnp.transpose(block_a)
    ct[...] = jnp.transpose(jnp.concatenate([c_all, jnp.zeros((120, 256), F32)], 0))
    c_t = split(ct[...])
    gcm[...] = dot3(c_t, c_t, NT)
    a_t_split = split(a_t)
    gam[...] = dot3(a_t_split, a_t_split, NT)
    for k in range(8):
        hi, lo = split(a_t * ct[:, k : k + 1])
        whi[:, k * 128 : (k + 1) * 128] = hi
        wlo[:, k * 128 : (k + 1) * 128] = lo

    def first(j, _):
        at = pl.ds(pl.multiple_of(j * 256, 256), 256)
        m1[:, at] = dot3((whi[...], wlo[...]), (thi[:, at], tlo[:, at]), NN)
        return 0

    arrive([on_up, on_down])
    far1 = stage1(far, bg.at[far, x, y])
    arrive(down1)
    down2 = stage2(down)
    arrive(up1)
    up2 = stage2(up)
    lax.fori_loop(0, 2, first, 0)
    arrive(far1)
    far2 = stage2(far)
    h_split = split(gam[...] * gcm[...])
    hm[0], hm[1] = h_split
    lax.fori_loop(2, 4, first, 0)
    arrive(own2 + down2 + up2 + far2)

    bg2 = bg.reshape(2048, 128)
    for j in range(8):
        for q in range(4):
            btn[j, pl.ds(q, 64, stride=4), :] = bg2[pl.ds(j * 4 + q, 64, stride=32), :]
        hi, lo = split(btn[j])
        bhi[:, j * 128 : (j + 1) * 128] = hi
        blo[:, j * 128 : (j + 1) * 128] = lo

    b_split = (bhi[...], blo[...])
    gbm[...] = dot3(b_split, b_split, NT)

    pa[...] = jnp.zeros_like(pa)

    def second(m, _):
        at = pl.ds(pl.multiple_of(m * 512, 512), 512)
        part = dot3((thi[at, :], tlo[at, :]), (bhi[...], blo[...]), NT)
        rows_a = ab[...].reshape(128, 256)
        acc = pa[...].reshape(128, 256)
        for k in range(4):
            one = part[k * 128 : (k + 1) * 128]
            acc = acc + one * c_ref[pl.ds(m * 4 + k, 1), :]
            pck[pl.ds(m * 4 + k, 1), :] = jnp.sum(one * rows_a, axis=0, keepdims=True)
        pa[...] = acc.reshape(4, 2, 16, 256)
        return 0

    lax.fori_loop(0, 2, second, 0)
    c_part = dot3(split(c_ref[...]), split(gam[...] * gbm[...]), NN) - pck[...]
    cown[0] = c_part[:, :128]
    cown[1] = c_part[:, 128:]
    c1 = send(cown.at[other], ccore, twin)

    def third(j, _):
        at = pl.ds(pl.multiple_of(j * 256, 256), 256)
        got = dot3((hm[0], hm[1]), (bhi[:, at], blo[:, at]), NN) - m1[:, at]
        btn[2 * j] = got[:, :128]
        btn[2 * j + 1] = got[:, 128:]
        return 0

    lax.fori_loop(0, 4, third, 0)
    gr2 = gr.reshape(2048, 128)
    for j in range(8):
        for q in range(4):
            gr2[pl.ds(j * 4 + q, 64, stride=32), :] = btn[j, pl.ds(q, 64, stride=4), :]

    def scatter1(n, w):
        return [
            send(gr.at[w, :, (y + d) % 4, 0], r1.at[n, 0, d - 1], yp(d))
            for d in (1, 2, 3)
        ] + [
            send(gr.at[w, (x + d) % 4, :, 1], r1.at[n, 1, d - 1], xp(d))
            for d in (1, 2, 3)
        ]

    def scatter2(n, w, copies):
        arrive(copies)
        gr[w, :, y, 0] = gr[w, :, y, 0] + r1[n, 0, 0] + r1[n, 0, 1] + r1[n, 0, 2]
        gr[w, x, :, 1] = gr[w, x, :, 1] + r1[n, 1, 0] + r1[n, 1, 1] + r1[n, 1, 2]
        return [
            send(gr.at[w, (x + d) % 4, y, 0], r2.at[n, 0, d - 1], xp(d))
            for d in (1, 2, 3)
        ] + [
            send(gr.at[w, x, (y + d) % 4, 1], r2.at[n, 1, d - 1], yp(d))
            for d in (1, 2, 3)
        ]

    def scattered(n, w, copies):
        arrive(copies)
        gr[w, x, y] = gr[w, x, y] + r2[n, :, 0] + r2[n, :, 1] + r2[n, :, 2]

    far_s = scatter1(0, far)
    up_s = scatter1(1, up)
    down_s = scatter1(2, down)
    own_s = scatter1(3, zh)

    c1.wait_recv()
    cx[x] = cown[core] + ccore[...]
    c2 = [send(cx.at[x], cx.at[x], xp(d)) for d in (1, 2, 3)]

    h = split(gbm[...] * gcm[...])
    got = dot3(split(ab[...].reshape(128, 256)), h, NN) - pa[...].reshape(128, 256)
    pa[...] = got.reshape(4, 2, 16, 256)
    p1 = send(pa.at[:, other], pcore, twin)

    arrive(c2)
    cy[y] = (cx[0] + cx[1]) + (cx[2] + cx[3])
    c3 = [send(cy.at[y], cy.at[y], yp(d)) for d in (1, 2, 3)]

    p1.wait_recv()
    psum[...] = pa[:, core] + pcore[...]
    p2 = [send(psum.at[(zl + d) % 4], pz.at[d - 1], lp(d)) for d in (1, 2, 3)]

    arrive(c3)
    cz[zl] = (cy[0] + cy[1]) + (cy[2] + cy[3])
    c4 = [send(cz.at[zl], cz.at[zl], lp(d)) for d in (1, 2, 3)]

    far_s = scatter2(0, far, far_s)
    up_s = scatter2(1, up, up_s)
    down_s = scatter2(2, down, down_s)

    arrive(c4)
    ch[0] = (cz[0] + cz[1]) + (cz[2] + cz[3])
    c5 = send(ch.at[0], ch.at[1], at_row(zh + 1 - 2 * (zh % 2), x, y))

    own_s = scatter2(3, zh, own_s)
    scattered(0, far, far_s)
    f_up = send(gr.at[far, x, y, 0], z1.at[0], zp(1))
    f_down = send(gr.at[far, x, y, 1], z1.at[1], zp(3))
    scattered(1, up, up_s)
    scattered(2, down, down_s)

    arrive(p2)
    ga_out[...] = psum[zl] + pz[0] + pz[1] + pz[2]

    c5.wait_recv()
    ch[2] = ch[0] + ch[1]
    c6 = send(ch.at[2], ch.at[3], at_row(3 - zh, x, y))

    f_up.wait_recv()
    gr[up, x, y, 0] = gr[up, x, y, 0] + z1[0]
    l_up = send(gr.at[up, x, y], z2.at[0], zp(1))
    f_down.wait_recv()
    gr[down, x, y, 1] = gr[down, x, y, 1] + z1[1]
    l_down = send(gr.at[down, x, y], z2.at[1], zp(3))
    scattered(3, zh, own_s)

    c6.wait_recv()
    cf[core] = ch[2] + ch[3]
    c7 = send(cf.at[core], cf.at[core], twin)

    arrive([l_up, l_down])
    gbt_out[...] = gr[zh, x, y] + z2[0] + z2[1]
    c7.wait_recv()
    gc_out[:, :128] = cf[0]
    gc_out[:, 128:] = cf[1]
    for copy in sent:
        copy.wait_send()


def local(tensor, factor_a, factor_bt, factor_c):
    bt = factor_bt.reshape(4, 8, 128).transpose(1, 0, 2).reshape(2, 16, 128)
    vmem = pl.BlockSpec(memory_space=pltpu.VMEM)
    grad_a, grad_bt, grad_c = pl.pallas_call(
        kernel,
        out_shape=(
            jax.ShapeDtypeStruct((16, 256), F32),
            jax.ShapeDtypeStruct((2, 16, 128), F32),
            jax.ShapeDtypeStruct((8, 256), F32),
        ),
        in_specs=[pl.BlockSpec(memory_space=pl.ANY), vmem, vmem, vmem],
        out_specs=(vmem, vmem, vmem),
        scratch_shapes=[
            pltpu.VMEM((8, 128, 1024), F32),
            pltpu.VMEM((1024, 1024), BF16),
            pltpu.VMEM((1024, 1024), BF16),
            pltpu.VMEM((256, 1024), BF16),
            pltpu.VMEM((256, 1024), BF16),
            pltpu.VMEM((256, 1024), F32),
            pltpu.VMEM((4, 2, 16, 256), F32),
            pltpu.VMEM((4, 4, 4, 2, 16, 128), F32),
            pltpu.VMEM((8, 256, 128), F32),
            pltpu.VMEM((256, 1024), BF16),
            pltpu.VMEM((256, 1024), BF16),
            pltpu.VMEM((2, 256, 256), BF16),
            pltpu.VMEM((256, 256), F32),
            pltpu.VMEM((256, 256), F32),
            pltpu.VMEM((256, 256), F32),
            pltpu.VMEM((4, 4, 4, 2, 16, 128), F32),
            pltpu.VMEM((4, 2, 3, 4, 16, 128), F32),
            pltpu.VMEM((4, 2, 3, 16, 128), F32),
            pltpu.VMEM((2, 16, 128), F32),
            pltpu.VMEM((2, 2, 16, 128), F32),
            pltpu.VMEM((4, 2, 16, 256), F32),
            pltpu.VMEM((4, 16, 256), F32),
            pltpu.VMEM((4, 16, 256), F32),
            pltpu.VMEM((3, 16, 256), F32),
            pltpu.VMEM((8, 256), F32),
            pltpu.VMEM((2, 8, 128), F32),
            pltpu.VMEM((8, 128), F32),
            pltpu.VMEM((4, 8, 128), F32),
            pltpu.VMEM((4, 8, 128), F32),
            pltpu.VMEM((4, 8, 128), F32),
            pltpu.VMEM((4, 8, 128), F32),
            pltpu.VMEM((2, 8, 128), F32),
            pltpu.VMEM((256, 128), F32),
            pltpu.SemaphoreType.DMA((NSEM,)),
            pltpu.SemaphoreType.DMA((NSEM,)),
            pltpu.SemaphoreType.DMA((3,)),
        ],
        compiler_params=pltpu.CompilerParams(collective_id=0, has_side_effects=True),
    )(tensor, factor_a, bt, factor_c)
    grad_bt = grad_bt.reshape(8, 4, 128).transpose(1, 0, 2).reshape(4, 1024)
    return grad_a, grad_bt, grad_c


def solution(mesh):
    in_specs = (P(None, "row", "col"), P(("row", "col"), None), P("row", "col"), P())
    out_specs = (P(("row", "col"), None), P("row", "col"), P())
    return jax.shard_map(local, mesh=mesh, in_specs=in_specs, out_specs=out_specs, check_vma=False)
```

```python
import jax
import jax.numpy as jnp
from jax import lax
from jax.experimental import pallas as pl
from jax.experimental.pallas import tpu as pltpu
from jax.sharding import PartitionSpec as P

MESH = pl.DeviceIdType.MESH
F32, BF16 = jnp.float32, jnp.bfloat16
NSEM = 176
NN = (((1,), (0,)), ((), ()))
NT = (((1,), (1,)), ((), ()))
PLANE = [(i, j) for i in range(4) for j in range(4) if i or j]


def split(v):
    hi = v.astype(BF16)
    return hi, (v - hi.astype(F32)).astype(BF16)


def dot3(a, b, dims):
    def one(u, v):
        return lax.dot_general(u, v, dims, preferred_element_type=F32)

    return one(a[0], b[0]) + (one(a[0], b[1]) + one(a[1], b[0]))


def added(parts):
    while len(parts) > 1:
        parts = [a + b for a, b in zip(parts[::2], parts[1::2])] + parts[len(parts) & ~1 :]
    return parts[0]


def kernel(
    t_hbm, a_hbm, bt_hbm, c_hbm,
    ga_hbm, gbt_hbm, gc_hbm,
    tf, thi, tlo, whi, wlo, m1, ab, bg, btn, bhi, blo, hm, gam, gcm, gbm,
    gr, r1, z1, z2, pa, pcore, psum, pz, pck, cp, cz, ch,
    cv, at, ct, ga_out, gbt_out, gc_out, ssem, rsem, lsem,
):
    row, col = lax.axis_index("row"), lax.axis_index("col")
    zh, x, y = row // 16, (row // 4) % 4, row % 4
    zl, core = col // 2, col % 2
    other = 1 - core
    here = x * 4 + y
    up, down, far = (zh + 1) % 4, (zh + 3) % 4, (zh + 2) % 4

    def pp(d):
        return (zh * 16 + ((x + d[0]) % 4) * 4 + (y + d[1]) % 4, col)

    def zp(d):
        return (((zh + d) % 4) * 16 + here, col)

    def lp(d, c):
        return (row, ((zl + d) % 4) * 2 + c)

    twin = (row, zl * 2 + other)
    column = [lp(d, c) for d in (1, 2, 3) for c in (core, other)] + [twin]
    sent = []

    def send(src, dst, device):
        k = len(sent)
        copy = pltpu.make_async_remote_copy(
            src_ref=src, dst_ref=dst, send_sem=ssem.at[k], recv_sem=rsem.at[k],
            device_id=device, device_id_type=MESH,
        )
        copy.start()
        sent.append(copy)
        return copy

    def arrive(copies):
        for copy in copies:
            copy.wait_recv()

    barrier = pltpu.get_barrier_semaphore()
    peers = [zp(1), zp(3)] + [pp(d) for d in PLANE] + column
    for device in peers:
        pl.semaphore_signal(barrier, inc=1, device_id=device, device_id_type=MESH)
    loads = [
        pltpu.make_async_copy(src, dst, lsem.at[k])
        for k, (src, dst) in enumerate(
            [(bt_hbm, bg.at[zh, x, y]), (a_hbm, ab.at[zl, core]), (c_hbm, cv), (t_hbm, tf)]
        )
    ]
    for load in loads:
        load.start()
    for load in loads[:3]:
        load.wait()
    pl.semaphore_wait(barrier, len(peers))

    def spread(w):
        mine = bg.at[w, x, y]
        return [send(mine, mine, pp(d)) for d in PLANE]

    mine = bg.at[zh, x, y]
    z_up = send(mine, mine, zp(1))
    z_down = send(mine, mine, zp(3))
    own_w = spread(zh)

    loads[3].wait()

    def split_t(k, _):
        hi, lo = split(tf[k])
        rows = pl.ds(pl.multiple_of(k * 128, 128), 128)
        thi[rows, :] = hi
        tlo[rows, :] = lo
        return 0

    lax.fori_loop(0, 8, split_t, 0)
    a_line = [send(ab.at[zl, core], ab.at[zl, core], lp(d, core)) for d in (1, 2, 3)]

    ct[...] = jnp.transpose(jnp.concatenate([cv[...], jnp.zeros((120, 256), F32)], 0))
    c_t = split(ct[...])
    gcm[...] = dot3(c_t, c_t, NT)

    def permuted(ref):
        return jnp.concatenate([ref[pl.ds(q, 64, stride=4), :] for q in range(4)], 0)

    ct_p = permuted(ct)

    z_up.wait_recv()
    half = bg.at[down, x, y, 0]
    on_up = send(half, half, zp(1))
    z_down.wait_recv()
    half = bg.at[up, x, y, 1]
    on_down = send(half, half, zp(3))
    down_w = spread(down)
    up_w = spread(up)

    arrive(a_line)
    a_twin = send(ab.at[:, core], ab.at[:, core], twin)

    bg2 = bg.reshape(2048, 128)

    def ordered(w, copies):
        arrive(copies)
        rows = pl.ds(pl.multiple_of(w * 64, 64), 64)
        for j in range(8):
            for q in range(4):
                btn[j, pl.ds(w * 64 + q, 16, stride=4), :] = bg2[
                    pl.ds(w * 512 + j * 4 + q, 16, stride=32), :
                ]
        for j in range(8):
            hi, lo = split(btn[j, rows, :])
            bhi[rows, j * 128 : (j + 1) * 128] = hi
            blo[rows, j * 128 : (j + 1) * 128] = lo

    ordered(zh, own_w)

    a_twin.wait_recv()
    at[...] = jnp.transpose(ab[...].reshape(128, 256))
    a_t = split(at[...])
    gam[...] = dot3(a_t, a_t, NT)
    at_p = permuted(at)
    h = dot3(split(at_p), a_t, NT) * dot3(split(ct_p), c_t, NT)
    hm[0], hm[1] = split(h)

    arrive([on_up, on_down])
    far_w = spread(far)

    for k in range(8):
        hi, lo = split(at_p * ct_p[:, k : k + 1])
        whi[:, k * 128 : (k + 1) * 128] = hi
        wlo[:, k * 128 : (k + 1) * 128] = lo

    def first(j, _):
        cols = pl.ds(pl.multiple_of(j * 256, 256), 256)
        m1[:, cols] = dot3((whi[...], wlo[...]), (thi[:, cols], tlo[:, cols]), NN)
        return 0

    lax.fori_loop(0, 4, first, 0)
    ordered(down, down_w)
    ordered(up, up_w)
    pa[...] = jnp.zeros_like(pa)
    arrive(far_w)
    ordered(far, [])

    b_split = (bhi[...], blo[...])
    gbm[...] = dot3(b_split, b_split, NT)

    def second(m, _):
        rows = pl.ds(pl.multiple_of(m * 512, 512), 512)
        part = dot3((thi[rows, :], tlo[rows, :]), (bhi[...], blo[...]), NT)
        rows_a = ab[...].reshape(128, 256)
        acc = pa[...].reshape(128, 256)
        for k in range(4):
            one = part[k * 128 : (k + 1) * 128]
            acc = acc + one * cv[pl.ds(m * 4 + k, 1), :]
            pck[pl.ds(m * 4 + k, 1), :] = jnp.sum(one * rows_a, axis=0, keepdims=True)
        pa[...] = acc.reshape(4, 2, 16, 256)
        return 0

    lax.fori_loop(0, 2, second, 0)
    cp[here] = dot3(split(cv[...]), split(gam[...] * gbm[...]), NN) - pck[...]
    c1 = [send(cp.at[here], cp.at[here], pp(d)) for d in PLANE]

    gr2 = gr.reshape(2048, 128)
    for j in range(4):
        cols = slice(j * 256, (j + 1) * 256)
        got = dot3((hm[0], hm[1]), (bhi[:, cols], blo[:, cols]), NN) - m1[:, cols]
        for i in range(2):
            for q in range(4):
                gr2[pl.ds((j * 2 + i) * 4 + q, 64, stride=32), :] = got[
                    q * 64 : (q + 1) * 64, i * 128 : (i + 1) * 128
                ]

    def scatter(n, w):
        return [
            send(gr.at[w, (x + d[0]) % 4, (y + d[1]) % 4], r1.at[n, i], pp(d))
            for i, d in enumerate(PLANE)
        ]

    def gathered(n, w, copies):
        arrive(copies)
        gr[w, x, y] = gr[w, x, y] + added([r1[n, i] for i in range(15)])

    far_s = scatter(0, far)
    up_s = scatter(1, up)
    down_s = scatter(2, down)

    h = split(gbm[...] * gcm[...])
    got = dot3(split(ab[...].reshape(128, 256)), h, NN) - pa[...].reshape(128, 256)
    pa[...] = got.reshape(4, 2, 16, 256)
    p1 = send(pa.at[:, other], pcore, twin)

    arrive(c1)
    cz[col] = added([cp[i] for i in range(16)])
    c2 = [send(cz.at[col], cz.at[col], device) for device in column]
    own_s = scatter(3, zh)

    p1.wait_recv()
    psum[...] = pa[:, core] + pcore[...]
    p2 = [send(psum.at[(zl + d) % 4], pz.at[d - 1], lp(d, core)) for d in (1, 2, 3)]

    gathered(0, far, far_s)
    f_up = send(gr.at[far, x, y, 0], z1.at[0], zp(1))
    f_down = send(gr.at[far, x, y, 1], z1.at[1], zp(3))

    arrive(c2)
    ch[zh] = added([cz[i] for i in range(8)])
    c3 = [send(ch.at[zh], ch.at[zh], zp(d)) for d in (2, 1, 3)]

    gathered(1, up, up_s)
    gathered(2, down, down_s)
    f_up.wait_recv()
    gr[up, x, y, 0] = gr[up, x, y, 0] + z1[0]
    l_up = send(gr.at[up, x, y], z2.at[0], zp(1))
    f_down.wait_recv()
    gr[down, x, y, 1] = gr[down, x, y, 1] + z1[1]
    l_down = send(gr.at[down, x, y], z2.at[1], zp(3))

    arrive(p2)
    ga_out[...] = psum[zl] + pz[0] + pz[1] + pz[2]
    stores = [pltpu.make_async_copy(ga_out, ga_hbm, lsem.at[0])]
    stores[0].start()
    gathered(3, zh, own_s)

    arrive([l_up, l_down])
    gbt_out[...] = gr[zh, x, y] + z2[0] + z2[1]
    stores.append(pltpu.make_async_copy(gbt_out, gbt_hbm, lsem.at[1]))
    stores[1].start()
    arrive(c3)
    gc_out[...] = added([ch[i] for i in range(4)])
    stores.append(pltpu.make_async_copy(gc_out, gc_hbm, lsem.at[2]))
    stores[2].start()
    for copy in sent:
        copy.wait_send()
    for store in stores:
        store.wait()


def last(a_in, b_in, c_in, a_out, b_out, c_out):
    a_out[...] = a_in[...]
    b_out[...] = b_in[...]
    c_out[...] = c_in[...]


def local(tensor, factor_a, factor_bt, factor_c):
    bt = factor_bt.reshape(4, 8, 128).transpose(1, 0, 2).reshape(2, 16, 128)
    shapes = (
        jax.ShapeDtypeStruct((16, 256), F32),
        jax.ShapeDtypeStruct((2, 16, 128), F32),
        jax.ShapeDtypeStruct((8, 256), F32),
    )
    anywhere, vmem = pl.BlockSpec(memory_space=pl.ANY), pl.BlockSpec(memory_space=pltpu.VMEM)
    parts = pl.pallas_call(
        kernel,
        out_shape=shapes,
        in_specs=[anywhere] * 4,
        out_specs=(anywhere,) * 3,
        scratch_shapes=[
            pltpu.VMEM((8, 128, 1024), F32),
            pltpu.VMEM((1024, 1024), BF16),
            pltpu.VMEM((1024, 1024), BF16),
            pltpu.VMEM((256, 1024), BF16),
            pltpu.VMEM((256, 1024), BF16),
            pltpu.VMEM((256, 1024), F32),
            pltpu.VMEM((4, 2, 16, 256), F32),
            pltpu.VMEM((4, 4, 4, 2, 16, 128), F32),
            pltpu.VMEM((8, 256, 128), F32),
            pltpu.VMEM((256, 1024), BF16),
            pltpu.VMEM((256, 1024), BF16),
            pltpu.VMEM((2, 256, 256), BF16),
            pltpu.VMEM((256, 256), F32),
            pltpu.VMEM((256, 256), F32),
            pltpu.VMEM((256, 256), F32),
            pltpu.VMEM((4, 4, 4, 2, 16, 128), F32),
            pltpu.VMEM((4, 15, 2, 16, 128), F32),
            pltpu.VMEM((2, 16, 128), F32),
            pltpu.VMEM((2, 2, 16, 128), F32),
            pltpu.VMEM((4, 2, 16, 256), F32),
            pltpu.VMEM((4, 16, 256), F32),
            pltpu.VMEM((4, 16, 256), F32),
            pltpu.VMEM((3, 16, 256), F32),
            pltpu.VMEM((8, 256), F32),
            pltpu.VMEM((16, 8, 256), F32),
            pltpu.VMEM((8, 8, 256), F32),
            pltpu.VMEM((4, 8, 256), F32),
            pltpu.VMEM((8, 256), F32),
            pltpu.VMEM((256, 128), F32),
            pltpu.VMEM((256, 128), F32),
            pltpu.VMEM((16, 256), F32),
            pltpu.VMEM((2, 16, 128), F32),
            pltpu.VMEM((8, 256), F32),
            pltpu.SemaphoreType.DMA((NSEM,)),
            pltpu.SemaphoreType.DMA((NSEM,)),
            pltpu.SemaphoreType.DMA((4,)),
        ],
        compiler_params=pltpu.CompilerParams(collective_id=0, has_side_effects=True),
    )(tensor, factor_a, bt, factor_c)
    grad_a, grad_bt, grad_c = pl.pallas_call(
        last, out_shape=shapes, in_specs=[vmem] * 3, out_specs=(vmem,) * 3
    )(*parts)
    grad_bt = grad_bt.reshape(8, 4, 128).transpose(1, 0, 2).reshape(4, 1024)
    return grad_a, grad_bt, grad_c


def solution(mesh):
    in_specs = (P(None, "row", "col"), P(("row", "col"), None), P("row", "col"), P())
    out_specs = (P(("row", "col"), None), P("row", "col"), P())
    return jax.shard_map(local, mesh=mesh, in_specs=in_specs, out_specs=out_specs, check_vma=False)
```

```python
import jax
import jax.numpy as jnp
from jax import lax
from jax.experimental import pallas as pl
from jax.experimental.pallas import tpu as pltpu
from jax.sharding import PartitionSpec as P

MESH = pl.DeviceIdType.MESH
F32, BF16 = jnp.float32, jnp.bfloat16
NSEM = 176
NN = (((1,), (0,)), ((), ()))
NT = (((1,), (1,)), ((), ()))
PLANE = sorted(
    ((i, j) for i in range(4) for j in range(4) if i or j),
    key=lambda d: -min(d[0], 4 - d[0]) - min(d[1], 4 - d[1]),
)


def split(v):
    hi = v.astype(BF16)
    return hi, (v - hi.astype(F32)).astype(BF16)


def dot3(a, b, dims):
    def one(u, v):
        return lax.dot_general(u, v, dims, preferred_element_type=F32)

    return one(a[0], b[0]) + (one(a[0], b[1]) + one(a[1], b[0]))


def added(parts):
    while len(parts) > 1:
        parts = [a + b for a, b in zip(parts[::2], parts[1::2])] + parts[len(parts) & ~1 :]
    return parts[0]


def kernel(
    t_hbm, a_hbm, bt_hbm, c_hbm,
    ga_res, gbt_res, gc_res,
    tf, thi, tlo, whi, wlo, ab, bg, btn, bhi, blo, gam, gcm, gbm,
    gr, r1a, r1b, r2a, r2b, z1a, z1b, z2, pa, pcore, psum, pz, pck, cp, cz, ch,
    cv, at, ct, ga_out, gbt_out, gc_out, ssem, rsem, lsem,
):
    row, col = lax.axis_index("row"), lax.axis_index("col")
    zh, x, y = row // 16, (row // 4) % 4, row % 4
    zl, core = col // 2, col % 2
    other = 1 - core
    here = x * 4 + y
    up, down, far = (zh + 1) % 4, (zh + 3) % 4, (zh + 2) % 4

    def pp(d):
        return (zh * 16 + ((x + d[0]) % 4) * 4 + (y + d[1]) % 4, col)

    def zp(d):
        return (((zh + d) % 4) * 16 + here, col)

    def lp(d, c):
        return (row, ((zl + d) % 4) * 2 + c)

    twin = (row, zl * 2 + other)
    column = [lp(d, c) for d in (1, 2, 3) for c in (core, other)] + [twin]
    sent = []

    def send(src, dst, device):
        k = len(sent)
        copy = pltpu.make_async_remote_copy(
            src_ref=src, dst_ref=dst, send_sem=ssem.at[k], recv_sem=rsem.at[k],
            device_id=device, device_id_type=MESH,
        )
        copy.start()
        sent.append(copy)
        return copy

    def arrive(copies):
        for copy in copies:
            copy.wait_recv()

    barrier = pltpu.get_barrier_semaphore()
    peers = [zp(1), zp(3)] + [pp(d) for d in PLANE] + column
    for device in peers:
        pl.semaphore_signal(barrier, inc=1, device_id=device, device_id_type=MESH)
    loads = [
        pltpu.make_async_copy(src, dst, lsem.at[k])
        for k, (src, dst) in enumerate(
            [(bt_hbm, bg.at[zh, x, y]), (a_hbm, ab.at[zl, core]), (c_hbm, cv), (t_hbm, tf)]
        )
    ]
    for load in loads:
        load.start()
    pl.semaphore_wait(barrier, len(peers))

    def spread(w, src):
        return [send(src, bg.at[w, x, y], pp(d)) for d in PLANE]

    z_up = [send(bt_hbm.at[0], bg.at[zh, x, y, 0], zp(1))]
    z_down = [send(bt_hbm.at[1], bg.at[zh, x, y, 1], zp(3))]
    z_up.append(send(bt_hbm.at[1], bg.at[zh, x, y, 1], zp(1)))
    z_down.append(send(bt_hbm.at[0], bg.at[zh, x, y, 0], zp(3)))
    own_w = spread(zh, bt_hbm)

    loads[3].wait()

    def split_t(k, _):
        hi, lo = split(tf[k])
        rows = pl.ds(pl.multiple_of(k * 128, 128), 128)
        thi[rows, :] = hi
        tlo[rows, :] = lo
        return 0

    lax.fori_loop(0, 8, split_t, 0)

    for load in loads[:3]:
        load.wait()
    ct[...] = jnp.transpose(jnp.concatenate([cv[...], jnp.zeros((120, 256), F32)], 0))
    c_t = split(ct[...])
    gcm[...] = dot3(c_t, c_t, NT)

    def permuted(ref):
        return jnp.concatenate([ref[pl.ds(q, 64, stride=4), :] for q in range(4)], 0)

    ct_p = permuted(ct)

    a_line = [send(a_hbm, ab.at[zl, core], lp(d, core)) for d in (1, 2, 3)]
    z_up[0].wait_recv()
    half = bg.at[down, x, y, 0]
    on_up = send(half, half, zp(1))
    z_down[0].wait_recv()
    half = bg.at[up, x, y, 1]
    on_down = send(half, half, zp(3))
    z_up[1].wait_recv()
    down_w = spread(down, bg.at[down, x, y])
    z_down[1].wait_recv()
    up_w = spread(up, bg.at[up, x, y])

    arrive(a_line)
    a_twin = send(ab.at[:, core], ab.at[:, core], twin)

    bg2 = bg.reshape(2048, 128)

    def ordered(w, copies):
        arrive(copies)
        rows = pl.ds(pl.multiple_of(w * 64, 64), 64)
        for j in range(8):
            for q in range(4):
                btn[j, pl.ds(w * 64 + q, 16, stride=4), :] = bg2[
                    pl.ds(w * 512 + j * 4 + q, 16, stride=32), :
                ]
        for j in range(8):
            hi, lo = split(btn[j, rows, :])
            bhi[rows, j * 128 : (j + 1) * 128] = hi
            blo[rows, j * 128 : (j + 1) * 128] = lo

    ordered(zh, own_w)

    a_twin.wait_recv()
    at[...] = jnp.transpose(ab[...].reshape(128, 256))
    a_t = split(at[...])
    gam[...] = dot3(a_t, a_t, NT)
    at_p = permuted(at)
    gr2 = gr.reshape(2560, 128)
    part = dot3(split(at_p), a_t, NT)
    for i in range(2):
        for q in range(4):
            gr2[pl.ds(32 + i * 4 + q, 64, stride=40), :] = part[
                q * 64 : (q + 1) * 64, i * 128 : (i + 1) * 128
            ]

    arrive([on_up, on_down])
    far_w = spread(far, bg.at[far, x, y])

    for k in range(8):
        hi, lo = split(at_p * ct_p[:, k : k + 1])
        whi[:, k * 128 : (k + 1) * 128] = hi
        wlo[:, k * 128 : (k + 1) * 128] = lo

    for j in range(4):
        cols = slice(j * 256, (j + 1) * 256)
        got = dot3((whi[...], wlo[...]), (thi[:, cols], tlo[:, cols]), NN)
        for i in range(2):
            for q in range(4):
                gr2[pl.ds((j * 2 + i) * 4 + q, 64, stride=40), :] = got[
                    q * 64 : (q + 1) * 64, i * 128 : (i + 1) * 128
                ]

    one, two = pl.ds(0, 2), pl.ds(2, 3)

    def scatter1(n, w):
        return [
            send(gr.at[w, :, (y + d) % 4, one], r1a.at[n, d - 1], pp((0, d)))
            for d in (2, 1, 3)
        ] + [
            send(gr.at[w, (x + d) % 4, :, two], r1b.at[n, d - 1], pp((d, 0)))
            for d in (2, 1, 3)
        ]

    def scatter2(n, w, copies):
        arrive(copies)
        gr[w, :, y, one] = gr[w, :, y, one] + added([r1a[n, i] for i in range(3)])
        gr[w, x, :, two] = gr[w, x, :, two] + added([r1b[n, i] for i in range(3)])
        return [
            send(gr.at[w, (x + d) % 4, y, one], r2a.at[n, d - 1], pp((d, 0)))
            for d in (2, 1, 3)
        ] + [
            send(gr.at[w, x, (y + d) % 4, two], r2b.at[n, d - 1], pp((0, d)))
            for d in (2, 1, 3)
        ]

    def gathered(n, w, copies):
        arrive(copies)
        gr[w, x, y, one] = gr[w, x, y, one] + added([r2a[n, i] for i in range(3)])
        gr[w, x, y, two] = gr[w, x, y, two] + added([r2b[n, i] for i in range(3)])

    ordered(down, down_w)
    ordered(up, up_w)
    pa[...] = jnp.zeros_like(pa)
    arrive(far_w)
    far_s = scatter1(0, far)
    ordered(far, [])
    up_s = scatter1(1, up)

    b_split = (bhi[...], blo[...])
    gbm[...] = dot3(b_split, b_split, NT)

    def second(m, _):
        rows = pl.ds(pl.multiple_of(m * 512, 512), 512)
        part = dot3((thi[rows, :], tlo[rows, :]), (bhi[...], blo[...]), NT)
        rows_a = ab[...].reshape(128, 256)
        acc = pa[...].reshape(128, 256)
        for k in range(4):
            one = part[k * 128 : (k + 1) * 128]
            acc = acc + one * cv[pl.ds(m * 4 + k, 1), :]
            pck[pl.ds(m * 4 + k, 1), :] = jnp.sum(one * rows_a, axis=0, keepdims=True)
        pa[...] = acc.reshape(4, 2, 16, 256)
        return 0

    lax.fori_loop(0, 2, second, 0)
    cp[here] = dot3(split(cv[...]), split(gam[...] * gbm[...]), NN) - pck[...]
    c1 = [send(cp.at[here], cp.at[here], pp(d)) for d in PLANE]

    down_s = scatter1(2, down)

    h = split(gbm[...] * gcm[...])
    got = dot3(split(ab[...].reshape(128, 256)), h, NN) - pa[...].reshape(128, 256)
    pa[...] = got.reshape(4, 2, 16, 256)
    p1 = send(pa.at[:, other], pcore, twin)

    far_s = scatter2(0, far, far_s)
    up_s = scatter2(1, up, up_s)

    arrive(c1)
    cz[col] = added([cp[i] for i in range(16)])
    c2 = [send(cz.at[col], cz.at[col], device) for device in column]
    down_s = scatter2(2, down, down_s)
    gathered(0, far, far_s)
    f_up = send(gr.at[far, x, y, one], z1a, zp(1))
    f_down = send(gr.at[far, x, y, two], z1b, zp(3))
    own_s = scatter1(3, zh)

    p1.wait_recv()
    psum[...] = pa[:, core] + pcore[...]
    p2 = [send(psum.at[(zl + d) % 4], pz.at[d - 1], lp(d, core)) for d in (1, 2, 3)]
    gathered(1, up, up_s)
    gathered(2, down, down_s)

    arrive(c2)
    ch[zh] = added([cz[i] for i in range(8)])
    c3 = [send(ch.at[zh], ch.at[zh], zp(d)) for d in (2, 1, 3)]

    f_up.wait_recv()
    gr[up, x, y, one] = gr[up, x, y, one] + z1a[...]
    l_up = send(gr.at[up, x, y], z2.at[0], zp(1))
    f_down.wait_recv()
    gr[down, x, y, two] = gr[down, x, y, two] + z1b[...]
    l_down = send(gr.at[down, x, y], z2.at[1], zp(3))
    own_s = scatter2(3, zh, own_s)

    arrive(p2)
    ga_out[...] = psum[zl] + pz[0] + pz[1] + pz[2]
    stores = [
        pltpu.make_async_copy(src, dst, lsem.at[k])
        for k, (src, dst) in enumerate([(ga_out, ga_res), (gbt_out, gbt_res), (gc_out, gc_res)])
    ]
    stores[0].start()
    gathered(3, zh, own_s)

    arrive([l_up, l_down])
    got = gr[zh, x, y] + z2[0] + z2[1]
    gram_a = jnp.concatenate([got[4, :4], got[4, 4:]], 1)
    gram_c = jnp.concatenate([gcm[pl.ds(row * 4 + q, 1), :] for q in range(4)], 0)
    h = jnp.concatenate([gram_a * gram_c, jnp.zeros((12, 256), F32)], 0)
    h = dot3(split(h), (bhi[...], blo[...]), NN)[:4]
    for t in range(4):
        two = [h[:, (2 * t + i) * 128 : (2 * t + i + 1) * 128] for i in range(2)]
        gbt_out[t] = jnp.concatenate(two, 0) - got[t]
    stores[1].start()
    arrive(c3)
    gc_out[...] = added([ch[i] for i in range(4)])
    stores[2].start()
    for copy in sent:
        copy.wait_send()
    for store in stores:
        store.wait()


def last(a_in, b_in, c_in, a_out, b_out, c_out):
    a_out[...] = a_in[...]
    b_out[...] = b_in[...]
    c_out[...] = c_in[...]


def local(tensor, factor_a, factor_bt, factor_c):
    bt = factor_bt.reshape(4, 8, 128).transpose(1, 0, 2).reshape(2, 16, 128)
    shapes = (
        jax.ShapeDtypeStruct((16, 256), F32),
        jax.ShapeDtypeStruct((4, 8, 128), F32),
        jax.ShapeDtypeStruct((8, 256), F32),
    )
    vmem = pl.BlockSpec(memory_space=pltpu.VMEM)
    parts = pl.pallas_call(
        kernel,
        out_shape=tuple(pltpu.VMEM(v.shape, v.dtype) for v in shapes),
        in_specs=[pl.BlockSpec(memory_space=pltpu.HBM)] * 4,
        out_specs=(pl.BlockSpec(memory_space=pl.ANY),) * 3,
        scratch_shapes=[
            pltpu.VMEM((8, 128, 1024), F32),
            pltpu.VMEM((1024, 1024), BF16),
            pltpu.VMEM((1024, 1024), BF16),
            pltpu.VMEM((256, 1024), BF16),
            pltpu.VMEM((256, 1024), BF16),
            pltpu.VMEM((4, 2, 16, 256), F32),
            pltpu.VMEM((4, 4, 4, 2, 16, 128), F32),
            pltpu.VMEM((8, 256, 128), F32),
            pltpu.VMEM((256, 1024), BF16),
            pltpu.VMEM((256, 1024), BF16),
            pltpu.VMEM((256, 256), F32),
            pltpu.VMEM((256, 256), F32),
            pltpu.VMEM((256, 256), F32),
            pltpu.VMEM((4, 4, 4, 5, 8, 128), F32),
            pltpu.VMEM((4, 3, 4, 2, 8, 128), F32),
            pltpu.VMEM((4, 3, 4, 3, 8, 128), F32),
            pltpu.VMEM((4, 3, 2, 8, 128), F32),
            pltpu.VMEM((4, 3, 3, 8, 128), F32),
            pltpu.VMEM((2, 8, 128), F32),
            pltpu.VMEM((3, 8, 128), F32),
            pltpu.VMEM((2, 5, 8, 128), F32),
            pltpu.VMEM((4, 2, 16, 256), F32),
            pltpu.VMEM((4, 16, 256), F32),
            pltpu.VMEM((4, 16, 256), F32),
            pltpu.VMEM((3, 16, 256), F32),
            pltpu.VMEM((8, 256), F32),
            pltpu.VMEM((16, 8, 256), F32),
            pltpu.VMEM((8, 8, 256), F32),
            pltpu.VMEM((4, 8, 256), F32),
            pltpu.VMEM((8, 256), F32),
            pltpu.VMEM((256, 128), F32),
            pltpu.VMEM((256, 128), F32),
            pltpu.VMEM((16, 256), F32),
            pltpu.VMEM((4, 8, 128), F32),
            pltpu.VMEM((8, 256), F32),
            pltpu.SemaphoreType.DMA((NSEM,)),
            pltpu.SemaphoreType.DMA((NSEM,)),
            pltpu.SemaphoreType.DMA((4,)),
        ],
        compiler_params=pltpu.CompilerParams(collective_id=0, has_side_effects=True),
    )(tensor, factor_a, bt, factor_c)
    grad_a, grad_bt, grad_c = pl.pallas_call(
        last, out_shape=shapes, in_specs=[vmem] * 3, out_specs=(vmem,) * 3
    )(*(pltpu.with_memory_space_constraint(v, pltpu.VMEM) for v in parts))
    grad_bt = grad_bt.reshape(8, 4, 128).transpose(1, 0, 2).reshape(4, 1024)
    return grad_a, grad_bt, grad_c


def solution(mesh):
    in_specs = (P(None, "row", "col"), P(("row", "col"), None), P("row", "col"), P())
    out_specs = (P(("row", "col"), None), P("row", "col"), P())
    return jax.shard_map(local, mesh=mesh, in_specs=in_specs, out_specs=out_specs, check_vma=False)
```

```python
import jax
import jax.numpy as jnp
from jax import lax
from jax.experimental import pallas as pl
from jax.experimental.pallas import tpu as pltpu
from jax.sharding import PartitionSpec as P

MESH = pl.DeviceIdType.MESH
F32, BF16 = jnp.float32, jnp.bfloat16
NSEM = 32
NN = (((1,), (0,)), ((), ()))
NT = (((1,), (1,)), ((), ()))
PLANE = sorted(
    ((i, j) for i in range(4) for j in range(4) if i or j),
    key=lambda d: -min(d[0], 4 - d[0]) - min(d[1], 4 - d[1]),
)


def split(v):
    hi = v.astype(BF16)
    return hi, (v - hi.astype(F32)).astype(BF16)


def dot3(a, b, dims):
    def one(u, v):
        return lax.dot_general(u, v, dims, preferred_element_type=F32)

    return one(a[0], b[0]) + (one(a[0], b[1]) + one(a[1], b[0]))


def added(parts):
    while len(parts) > 1:
        parts = [a + b for a, b in zip(parts[::2], parts[1::2])] + parts[len(parts) & ~1 :]
    return parts[0]


def kernel(
    t_hbm, a_hbm, bt_hbm, c_hbm,
    ga_res, gbt_res, gc_res,
    tf, thi, tlo, whi, wlo, ab, bg, btn, gam, gcm, gbm,
    gr, r1a, r1b, r2a, r2b, z1a, z1b, z2, pa, pcore, psum, pz, pck, cp, cz, ch,
    cv, at, ct, ga_out, gbt_out, gc_out, ssem, rsem, lsem,
):
    row, col = lax.axis_index("row"), lax.axis_index("col")
    zh, x, y = row // 16, (row // 4) % 4, row % 4
    zl, core = col // 2, col % 2
    other = 1 - core
    here = x * 4 + y
    up, down, far = (zh + 1) % 4, (zh + 3) % 4, (zh + 2) % 4

    def pp(d):
        return (zh * 16 + ((x + d[0]) % 4) * 4 + (y + d[1]) % 4, col)

    def zp(d):
        return (((zh + d) % 4) * 16 + here, col)

    def lp(d, c):
        return (row, ((zl + d) % 4) * 2 + c)

    twin = (row, zl * 2 + other)
    column = [lp(d, c) for d in (1, 2, 3) for c in (core, other)] + [twin]
    groups = []
    slots = bg.reshape(64, 2, 16, 128).at[pl.ds(0, 15)]

    def send(copies, sized):
        k = len(groups)
        groups.append(sized)
        for src, dst, device in copies:
            pltpu.make_async_remote_copy(
                src_ref=src, dst_ref=dst, send_sem=ssem.at[k], recv_sem=rsem.at[k],
                device_id=device, device_id_type=MESH,
            ).start()
        return k

    def arrive(*ks):
        for k in ks:
            pltpu.make_async_copy(groups[k], groups[k], rsem.at[k]).wait()

    barrier = pltpu.get_barrier_semaphore()
    peers = [zp(1), zp(3)] + [pp(d) for d in PLANE] + column
    for device in peers:
        pl.semaphore_signal(barrier, inc=1, device_id=device, device_id_type=MESH)
    loads = [
        pltpu.make_async_copy(src, dst, lsem.at[k])
        for k, (src, dst) in enumerate(
            [(bt_hbm, bg.at[zh, x, y]), (a_hbm, ab.at[zl, core]), (c_hbm, cv), (t_hbm, tf)]
        )
    ]
    for load in loads:
        load.start()
    pl.semaphore_wait(barrier, len(peers))

    def spread(w, src):
        return send([(src, bg.at[w, x, y], pp(d)) for d in PLANE], slots)

    h0, h1 = bg.at[zh, x, y, 0], bg.at[zh, x, y, 1]
    z_up0 = send([(bt_hbm.at[0], h0, zp(1))], h0)
    z_down1 = send([(bt_hbm.at[1], h1, zp(3))], h1)
    z_up1 = send([(bt_hbm.at[1], h1, zp(1))], h1)
    z_down0 = send([(bt_hbm.at[0], h0, zp(3))], h0)
    own_w = spread(zh, bt_hbm)

    loads[3].wait()

    def split_t(k, _):
        hi, lo = split(tf[k])
        rows = pl.ds(pl.multiple_of(k * 128, 128), 128)
        thi[rows, :] = hi
        tlo[rows, :] = lo
        return 0

    lax.fori_loop(0, 8, split_t, 0)

    for load in loads[:3]:
        load.wait()
    ct[...] = jnp.transpose(jnp.concatenate([cv[...], jnp.zeros((120, 256), F32)], 0))
    c_t = split(ct[...])
    gcm[...] = dot3(c_t, c_t, NT)

    def permuted(ref):
        return jnp.concatenate([ref[pl.ds(q, 64, stride=4), :] for q in range(4)], 0)

    ct_p = permuted(ct)

    a_line = send(
        [(a_hbm, ab.at[zl, core], lp(d, core)) for d in (1, 2, 3)],
        ab.reshape(8, 16, 256).at[pl.ds(0, 3)],
    )
    arrive(z_up0)
    half = bg.at[down, x, y, 0]
    on_up = send([(half, half, zp(1))], half)
    arrive(z_down1)
    half = bg.at[up, x, y, 1]
    on_down = send([(half, half, zp(3))], half)
    arrive(z_down0)
    up_1 = send(
        [(bg.at[up, x, y, 0], bg.at[up, x, y, 0], pp((d, 0))) for d in (2, 1, 3)]
        + [(bg.at[up, x, y, 1], bg.at[up, x, y, 1], pp((0, d))) for d in (2, 1, 3)],
        bg.reshape(64, 2, 16, 128).at[pl.ds(0, 3)],
    )
    arrive(z_up1)
    down_w = spread(down, bg.at[down, x, y])

    arrive(a_line)
    half = ab.at[:, core]
    a_twin = send([(half, half, twin)], half)

    bg2 = bg.reshape(2048, 128)

    def ordered(w, *copies):
        arrive(*copies)
        rows = pl.ds(pl.multiple_of(w * 64, 64), 64)
        below = pl.ds(pl.multiple_of(1024 + w * 64, 64), 64)
        for j in range(8):
            for q in range(4):
                btn[j, pl.ds(w * 64 + q, 16, stride=4), :] = bg2[
                    pl.ds(w * 512 + j * 4 + q, 16, stride=32), :
                ]
        for j in range(8):
            hi, lo = split(btn[j, rows, :])
            thi[below, j * 128 : (j + 1) * 128] = hi
            tlo[below, j * 128 : (j + 1) * 128] = lo

    ordered(zh, own_w)

    arrive(a_twin)
    at[...] = jnp.transpose(ab[...].reshape(128, 256))
    a_t = split(at[...])
    gam[...] = dot3(a_t, a_t, NT)
    at_p = permuted(at)
    gr2 = gr.reshape(2560, 128)
    part = dot3(split(at_p), a_t, NT)
    for i in range(2):
        for q in range(4):
            gr2[pl.ds(32 + i * 4 + q, 64, stride=40), :] = part[
                q * 64 : (q + 1) * 64, i * 128 : (i + 1) * 128
            ]

    arrive(up_1)
    up_w = send(
        [(bg.at[up, :, y, 0], bg.at[up, :, y, 0], pp((0, d))) for d in (2, 1, 3)]
        + [(bg.at[up, x, :, 1], bg.at[up, x, :, 1], pp((d, 0))) for d in (2, 1, 3)],
        bg.reshape(64, 2, 16, 128).at[pl.ds(0, 12)],
    )
    arrive(on_up, on_down)
    far_w = spread(far, bg.at[far, x, y])

    for k in range(8):
        hi, lo = split(at_p * ct_p[:, k : k + 1])
        whi[:, k * 128 : (k + 1) * 128] = hi
        wlo[:, k * 128 : (k + 1) * 128] = lo

    for j in range(4):
        cols = slice(j * 256, (j + 1) * 256)
        got = dot3((whi[...], wlo[...]), (thi[:1024, cols], tlo[:1024, cols]), NN)
        for i in range(2):
            for q in range(4):
                gr2[pl.ds((j * 2 + i) * 4 + q, 64, stride=40), :] = got[
                    q * 64 : (q + 1) * 64, i * 128 : (i + 1) * 128
                ]

    one, two = pl.ds(0, 2), pl.ds(2, 3)

    def scatter1(n, w):
        return send(
            [(gr.at[w, :, (y + d) % 4, one], r1a.at[n, d - 1], pp((0, d))) for d in (2, 1, 3)]
            + [(gr.at[w, (x + d) % 4, :, two], r1b.at[n, d - 1], pp((d, 0))) for d in (2, 1, 3)],
            slots,
        )

    def scatter2(n, w, copies):
        arrive(copies)
        gr[w, :, y, one] = gr[w, :, y, one] + added([r1a[n, i] for i in range(3)])
        gr[w, x, :, two] = gr[w, x, :, two] + added([r1b[n, i] for i in range(3)])
        return send(
            [(gr.at[w, (x + d) % 4, y, one], r2a.at[n, d - 1], pp((d, 0))) for d in (2, 1, 3)]
            + [(gr.at[w, x, (y + d) % 4, two], r2b.at[n, d - 1], pp((0, d))) for d in (2, 1, 3)],
            gr.reshape(64, 5, 8, 128).at[pl.ds(0, 3)],
        )

    def gathered(n, w, copies):
        arrive(copies)
        gr[w, x, y, one] = gr[w, x, y, one] + added([r2a[n, i] for i in range(3)])
        gr[w, x, y, two] = gr[w, x, y, two] + added([r2b[n, i] for i in range(3)])

    ordered(down, down_w)
    ordered(up, up_w)
    arrive(far_w)
    far_s = scatter1(0, far)
    ordered(far)
    up_s = scatter1(1, up)

    b_all = (thi[1024:1280], tlo[1024:1280])
    rows_a = ab[...].reshape(128, 256)
    acc = None
    for m in range(2):
        rows = slice(m * 640, (m + 1) * 640)
        part = dot3((thi[rows], tlo[rows]), b_all, NT)
        for k in range(5 if m == 0 else 3):
            one_k, at_k = part[k * 128 : (k + 1) * 128], m * 5 + k
            term = one_k * cv[at_k : at_k + 1]
            acc = term if acc is None else acc + term
            pck[at_k : at_k + 1] = jnp.sum(one_k * rows_a, axis=0, keepdims=True)
    gbm[...] = part[384:]
    pa[...] = acc.reshape(4, 2, 16, 256)
    cp[here] = dot3(split(cv[...]), split(gam[...] * gbm[...]), NN) - pck[...]
    c1 = send([(cp.at[here], cp.at[here], pp(d)) for d in PLANE], cp.at[pl.ds(0, 15)])

    h = split(gbm[...] * gcm[...])
    got = dot3(split(ab[...].reshape(128, 256)), h, NN) - pa[...].reshape(128, 256)
    pa[...] = got.reshape(4, 2, 16, 256)
    p1 = send([(pa.at[:, other], pcore, twin)], pcore)

    far_s = scatter2(0, far, far_s)
    down_s = scatter1(2, down)

    arrive(c1)
    cz[col] = added([cp[i] for i in range(16)])
    c2 = send([(cz.at[col], cz.at[col], device) for device in column], cz.at[pl.ds(0, 7)])
    gathered(0, far, far_s)
    f_up = send([(gr.at[far, x, y, one], z1a, zp(1))], z1a)
    f_down = send([(gr.at[far, x, y, two], z1b, zp(3))], z1b)

    arrive(p1)
    psum[...] = pa[:, core] + pcore[...]
    p2 = send([(psum.at[(zl + d) % 4], pz.at[d - 1], lp(d, core)) for d in (1, 2, 3)], pz)
    up_s = scatter2(1, up, up_s)
    down_s = scatter2(2, down, down_s)
    own_s = scatter1(3, zh)

    arrive(c2)
    ch[zh] = added([cz[i] for i in range(8)])
    c3 = send([(ch.at[zh], ch.at[zh], zp(d)) for d in (2, 1, 3)], ch.at[pl.ds(0, 3)])
    gathered(1, up, up_s)
    arrive(f_up)
    gr[up, x, y, one] = gr[up, x, y, one] + z1a[...]
    l_up = send([(gr.at[up, x, y], z2.at[0], zp(1))], z2.at[0])
    gathered(2, down, down_s)
    arrive(f_down)
    gr[down, x, y, two] = gr[down, x, y, two] + z1b[...]
    l_down = send([(gr.at[down, x, y], z2.at[1], zp(3))], z2.at[1])
    own_s = scatter2(3, zh, own_s)

    arrive(p2)
    ga_out[...] = psum[zl] + pz[0] + pz[1] + pz[2]
    stores = [
        pltpu.make_async_copy(src, dst, lsem.at[k])
        for k, (src, dst) in enumerate([(ga_out, ga_res), (gbt_out, gbt_res), (gc_out, gc_res)])
    ]
    stores[0].start()
    gathered(3, zh, own_s)

    arrive(l_up, l_down)
    got = gr[zh, x, y] + z2[0] + z2[1]
    gram_a = jnp.concatenate([got[4, :4], got[4, 4:]], 1)
    gram_c = jnp.concatenate([gcm[pl.ds(row * 4 + q, 1), :] for q in range(4)], 0)
    h = jnp.concatenate([gram_a * gram_c, jnp.zeros((12, 256), F32)], 0)
    h = dot3(split(h), (thi[1024:1280], tlo[1024:1280]), NN)[:4]
    for t in range(4):
        two = [h[:, (2 * t + i) * 128 : (2 * t + i + 1) * 128] for i in range(2)]
        gbt_out[t] = jnp.concatenate(two, 0) - got[t]
    stores[1].start()
    arrive(c3)
    gc_out[...] = added([ch[i] for i in range(4)])
    stores[2].start()
    for k, sized in enumerate(groups):
        pltpu.make_async_copy(sized, sized, ssem.at[k]).wait()
    for store in stores:
        store.wait()


def last(a_in, b_in, c_in, a_out, b_out, c_out):
    a_out[...] = a_in[...]
    b_out[...] = b_in[...]
    c_out[...] = c_in[...]


def local(tensor, factor_a, factor_bt, factor_c):
    bt = factor_bt.reshape(4, 8, 128).transpose(1, 0, 2).reshape(2, 16, 128)
    shapes = (
        jax.ShapeDtypeStruct((16, 256), F32),
        jax.ShapeDtypeStruct((4, 8, 128), F32),
        jax.ShapeDtypeStruct((8, 256), F32),
    )
    vmem = pl.BlockSpec(memory_space=pltpu.VMEM)
    parts = pl.pallas_call(
        kernel,
        out_shape=tuple(pltpu.VMEM(v.shape, v.dtype) for v in shapes),
        in_specs=[pl.BlockSpec(memory_space=pltpu.HBM)] * 4,
        out_specs=(pl.BlockSpec(memory_space=pl.ANY),) * 3,
        scratch_shapes=[
            pltpu.VMEM((8, 128, 1024), F32),
            pltpu.VMEM((1280, 1024), BF16),
            pltpu.VMEM((1280, 1024), BF16),
            pltpu.VMEM((256, 1024), BF16),
            pltpu.VMEM((256, 1024), BF16),
            pltpu.VMEM((4, 2, 16, 256), F32),
            pltpu.VMEM((4, 4, 4, 2, 16, 128), F32),
            pltpu.VMEM((8, 256, 128), F32),
            pltpu.VMEM((256, 256), F32),
            pltpu.VMEM((256, 256), F32),
            pltpu.VMEM((256, 256), F32),
            pltpu.VMEM((4, 4, 4, 5, 8, 128), F32),
            pltpu.VMEM((4, 3, 4, 2, 8, 128), F32),
            pltpu.VMEM((4, 3, 4, 3, 8, 128), F32),
            pltpu.VMEM((4, 3, 2, 8, 128), F32),
            pltpu.VMEM((4, 3, 3, 8, 128), F32),
            pltpu.VMEM((2, 8, 128), F32),
            pltpu.VMEM((3, 8, 128), F32),
            pltpu.VMEM((2, 5, 8, 128), F32),
            pltpu.VMEM((4, 2, 16, 256), F32),
            pltpu.VMEM((4, 16, 256), F32),
            pltpu.VMEM((4, 16, 256), F32),
            pltpu.VMEM((3, 16, 256), F32),
            pltpu.VMEM((8, 256), F32),
            pltpu.VMEM((16, 8, 256), F32),
            pltpu.VMEM((8, 8, 256), F32),
            pltpu.VMEM((4, 8, 256), F32),
            pltpu.VMEM((8, 256), F32),
            pltpu.VMEM((256, 128), F32),
            pltpu.VMEM((256, 128), F32),
            pltpu.VMEM((16, 256), F32),
            pltpu.VMEM((4, 8, 128), F32),
            pltpu.VMEM((8, 256), F32),
            pltpu.SemaphoreType.DMA((NSEM,)),
            pltpu.SemaphoreType.DMA((NSEM,)),
            pltpu.SemaphoreType.DMA((4,)),
        ],
        compiler_params=pltpu.CompilerParams(collective_id=0, has_side_effects=True),
    )(tensor, factor_a, bt, factor_c)
    grad_a, grad_bt, grad_c = pl.pallas_call(
        last, out_shape=shapes, in_specs=[vmem] * 3, out_specs=(vmem,) * 3
    )(*(pltpu.with_memory_space_constraint(v, pltpu.VMEM) for v in parts))
    grad_bt = grad_bt.reshape(8, 4, 128).transpose(1, 0, 2).reshape(4, 1024)
    return grad_a, grad_bt, grad_c


def solution(mesh):
    in_specs = (P(None, "row", "col"), P(("row", "col"), None), P("row", "col"), P())
    out_specs = (P(("row", "col"), None), P("row", "col"), P())
    return jax.shard_map(local, mesh=mesh, in_specs=in_specs, out_specs=out_specs, check_vma=False)
```

```python
import jax
import jax.numpy as jnp
from jax import lax
from jax.experimental import pallas as pl
from jax.experimental.pallas import tpu as pltpu
from jax.sharding import PartitionSpec as P

MESH = pl.DeviceIdType.MESH
F32, BF16 = jnp.float32, jnp.bfloat16
NSEM = 32
NN = (((1,), (0,)), ((), ()))
NT = (((1,), (1,)), ((), ()))
PLANE = sorted(
    ((i, j) for i in range(4) for j in range(4) if i or j),
    key=lambda d: -min(d[0], 4 - d[0]) - min(d[1], 4 - d[1]),
)


def split(v):
    hi = v.astype(BF16)
    return hi, (v - hi.astype(F32)).astype(BF16)


def dot3(a, b, dims):
    def one(u, v):
        return lax.dot_general(u, v, dims, preferred_element_type=F32)

    return one(a[0], b[0]) + (one(a[0], b[1]) + one(a[1], b[0]))


def added(parts):
    while len(parts) > 1:
        parts = [a + b for a, b in zip(parts[::2], parts[1::2])] + parts[len(parts) & ~1 :]
    return parts[0]


def kernel(
    t_hbm, a_hbm, bt_hbm, c_hbm,
    ga_res, gbt_res, gc_res,
    tf, thi, tlo, whi, wlo, ab, bg, btn, gam, gcm, gbm,
    gr, r1a, r1b, r2a, r2b, z1a, z1b, z2, pa, pcore, psum, pz, pck, cp, cz, ch,
    cv, at, ct, ga_out, gbt_out, gc_out, ssem, rsem, lsem,
):
    row, col = lax.axis_index("row"), lax.axis_index("col")
    zh, x, y = row // 16, (row // 4) % 4, row % 4
    zl, core = col // 2, col % 2
    other = 1 - core
    here = x * 4 + y
    up, down, far = (zh + 1) % 4, (zh + 3) % 4, (zh + 2) % 4

    def pp(d):
        return (zh * 16 + ((x + d[0]) % 4) * 4 + (y + d[1]) % 4, col)

    def zp(d):
        return (((zh + d) % 4) * 16 + here, col)

    def lp(d, c):
        return (row, ((zl + d) % 4) * 2 + c)

    twin = (row, zl * 2 + other)
    column = [lp(d, c) for d in (1, 2, 3) for c in (core, other)] + [twin]
    groups = []
    slots = bg.reshape(64, 2, 16, 128).at[pl.ds(0, 15)]

    def send(copies, sized):
        k = len(groups)
        groups.append(sized)
        for src, dst, device in copies:
            pltpu.make_async_remote_copy(
                src_ref=src, dst_ref=dst, send_sem=ssem.at[k], recv_sem=rsem.at[k],
                device_id=device, device_id_type=MESH,
            ).start()
        return k

    def arrive(*ks):
        for k in ks:
            pltpu.make_async_copy(groups[k], groups[k], rsem.at[k]).wait()

    barrier = pltpu.get_barrier_semaphore()
    peers = [zp(1), zp(3)] + [pp(d) for d in PLANE] + column
    for device in peers:
        pl.semaphore_signal(barrier, inc=1, device_id=device, device_id_type=MESH)
    loads = [
        pltpu.make_async_copy(src, dst, lsem.at[k])
        for k, (src, dst) in enumerate(
            [(bt_hbm, bg.at[zh, x, y]), (a_hbm, ab.at[zl, core]), (c_hbm, cv), (t_hbm, tf)]
        )
    ]
    for load in loads:
        load.start()
    pl.semaphore_wait(barrier, len(peers))

    def spread(w, src):
        return send([(src, bg.at[w, x, y], pp(d)) for d in PLANE], slots)

    h0, h1 = bg.at[zh, x, y, 0], bg.at[zh, x, y, 1]
    z_up0 = send([(bt_hbm.at[0], h0, zp(1))], h0)
    z_down1 = send([(bt_hbm.at[1], h1, zp(3))], h1)
    z_up1 = send([(bt_hbm.at[1], h1, zp(1))], h1)
    z_down0 = send([(bt_hbm.at[0], h0, zp(3))], h0)
    own_w = spread(zh, bt_hbm)

    loads[3].wait()

    def split_t(k, _):
        hi, lo = split(tf[k])
        rows = pl.ds(pl.multiple_of(k * 128, 128), 128)
        thi[rows, :] = hi
        tlo[rows, :] = lo
        return 0

    lax.fori_loop(0, 8, split_t, 0)

    for load in loads[:3]:
        load.wait()
    ct[...] = jnp.transpose(jnp.concatenate([cv[...], jnp.zeros((120, 256), F32)], 0))
    c_t = split(ct[...])
    gcm[...] = dot3(c_t, c_t, NT)

    def permuted(ref):
        return jnp.concatenate([ref[pl.ds(q, 64, stride=4), :] for q in range(4)], 0)

    ct_p = permuted(ct)

    a_line = send(
        [(a_hbm, ab.at[zl, core], lp(d, core)) for d in (1, 2, 3)],
        ab.reshape(8, 16, 256).at[pl.ds(0, 3)],
    )
    arrive(z_up0)
    half = bg.at[down, x, y, 0]
    on_up = send([(half, half, zp(1))], half)
    arrive(z_down1)
    half = bg.at[up, x, y, 1]
    on_down = send([(half, half, zp(3))], half)
    arrive(z_down0)
    up_1 = send(
        [(bg.at[up, x, y, 0], bg.at[up, x, y, 0], pp((d, 0))) for d in (2, 1, 3)]
        + [(bg.at[up, x, y, 1], bg.at[up, x, y, 1], pp((0, d))) for d in (2, 1, 3)],
        bg.reshape(64, 2, 16, 128).at[pl.ds(0, 3)],
    )
    arrive(z_up1)
    down_w = spread(down, bg.at[down, x, y])

    arrive(a_line)
    half = ab.at[:, core]
    a_twin = send([(half, half, twin)], half)

    bg2 = bg.reshape(2048, 128)

    def ordered(w, *copies):
        arrive(*copies)
        rows = pl.ds(pl.multiple_of(w * 64, 64), 64)
        below = pl.ds(pl.multiple_of(1024 + w * 64, 64), 64)
        for j in range(8):
            for q in range(4):
                btn[j, pl.ds(w * 64 + q, 16, stride=4), :] = bg2[
                    pl.ds(w * 512 + j * 4 + q, 16, stride=32), :
                ]
        for j in range(8):
            hi, lo = split(btn[j, rows, :])
            thi[below, j * 128 : (j + 1) * 128] = hi
            tlo[below, j * 128 : (j + 1) * 128] = lo

    ordered(zh, own_w)

    arrive(a_twin)
    at[...] = jnp.transpose(ab[...].reshape(128, 256))
    a_t = split(at[...])
    gam[...] = dot3(a_t, a_t, NT)
    at_p = permuted(at)
    gr2 = gr.reshape(2560, 128)
    part = dot3(split(at_p), a_t, NT)
    for i in range(2):
        for q in range(4):
            gr2[pl.ds(32 + i * 4 + q, 64, stride=40), :] = part[
                q * 64 : (q + 1) * 64, i * 128 : (i + 1) * 128
            ]

    arrive(up_1)
    up_w = send(
        [(bg.at[up, :, y, 0], bg.at[up, :, y, 0], pp((0, d))) for d in (2, 1, 3)]
        + [(bg.at[up, x, :, 1], bg.at[up, x, :, 1], pp((d, 0))) for d in (2, 1, 3)],
        bg.reshape(64, 2, 16, 128).at[pl.ds(0, 12)],
    )
    arrive(on_up, on_down)
    far_w = spread(far, bg.at[far, x, y])

    for k in range(8):
        hi, lo = split(at_p * ct_p[:, k : k + 1])
        whi[:, k * 128 : (k + 1) * 128] = hi
        wlo[:, k * 128 : (k + 1) * 128] = lo

    for j in range(4):
        cols = slice(j * 256, (j + 1) * 256)
        got = dot3((whi[...], wlo[...]), (thi[:1024, cols], tlo[:1024, cols]), NN)
        for i in range(2):
            for q in range(4):
                gr2[pl.ds((j * 2 + i) * 4 + q, 64, stride=40), :] = got[
                    q * 64 : (q + 1) * 64, i * 128 : (i + 1) * 128
                ]

    one, two = pl.ds(0, 2), pl.ds(2, 3)

    def parts_of(n):
        first, second = (one, r1a, r2a), (two, r1b, r2b)
        return (first, second) if n % 2 == 0 else (second, first)

    def scatter1(n, w):
        (ty, y1, _), (tx, x1, _) = parts_of(n)
        return send(
            [(gr.at[w, :, (y + d) % 4, ty], y1.at[n, d - 1], pp((0, d))) for d in (2, 1, 3)]
            + [(gr.at[w, (x + d) % 4, :, tx], x1.at[n, d - 1], pp((d, 0))) for d in (2, 1, 3)],
            slots,
        )

    def scatter2(n, w, copies):
        arrive(copies)
        (ty, y1, y2), (tx, x1, x2) = parts_of(n)
        gr[w, :, y, ty] = gr[w, :, y, ty] + added([y1[n, i] for i in range(3)])
        gr[w, x, :, tx] = gr[w, x, :, tx] + added([x1[n, i] for i in range(3)])
        return send(
            [(gr.at[w, (x + d) % 4, y, ty], y2.at[n, d - 1], pp((d, 0))) for d in (2, 1, 3)]
            + [(gr.at[w, x, (y + d) % 4, tx], x2.at[n, d - 1], pp((0, d))) for d in (2, 1, 3)],
            gr.reshape(64, 5, 8, 128).at[pl.ds(0, 3)],
        )

    def gathered(n, w, copies):
        arrive(copies)
        (ty, _, y2), (tx, _, x2) = parts_of(n)
        gr[w, x, y, ty] = gr[w, x, y, ty] + added([y2[n, i] for i in range(3)])
        gr[w, x, y, tx] = gr[w, x, y, tx] + added([x2[n, i] for i in range(3)])

    ordered(down, down_w)
    ordered(up, up_w)
    arrive(far_w)
    far_s = scatter1(0, far)
    ordered(far)

    b_all = (thi[1024:1280], tlo[1024:1280])
    rows_a = ab[...].reshape(128, 256)
    acc = None
    for m in range(2):
        rows = slice(m * 640, (m + 1) * 640)
        part = dot3((thi[rows], tlo[rows]), b_all, NT)
        for k in range(5 if m == 0 else 3):
            one_k, at_k = part[k * 128 : (k + 1) * 128], m * 5 + k
            term = one_k * cv[at_k : at_k + 1]
            acc = term if acc is None else acc + term
            pck[at_k : at_k + 1] = jnp.sum(one_k * rows_a, axis=0, keepdims=True)
    gbm[...] = part[384:]
    pa[...] = acc.reshape(4, 2, 16, 256)
    cp[here] = dot3(split(cv[...]), split(gam[...] * gbm[...]), NN) - pck[...]
    c1 = send([(cp.at[here], cp.at[here], pp(d)) for d in PLANE], cp.at[pl.ds(0, 15)])

    h = split(gbm[...] * gcm[...])
    got = dot3(split(ab[...].reshape(128, 256)), h, NN) - pa[...].reshape(128, 256)
    pa[...] = got.reshape(4, 2, 16, 256)
    p1 = send([(pa.at[:, other], pcore, twin)], pcore)

    far_s = scatter2(0, far, far_s)
    up_s = scatter1(1, up)
    down_s = scatter1(2, down)

    arrive(c1)
    cz[col] = added([cp[i] for i in range(16)])
    c2 = send([(cz.at[col], cz.at[col], device) for device in column], cz.at[pl.ds(0, 7)])
    gathered(0, far, far_s)
    f_up = send([(gr.at[far, x, y, one], z1a, zp(1))], z1a)
    f_down = send([(gr.at[far, x, y, two], z1b, zp(3))], z1b)

    arrive(p1)
    psum[...] = pa[:, core] + pcore[...]
    p2 = send([(psum.at[(zl + d) % 4], pz.at[d - 1], lp(d, core)) for d in (1, 2, 3)], pz)
    up_s = scatter2(1, up, up_s)
    down_s = scatter2(2, down, down_s)
    own_s = scatter1(3, zh)

    arrive(c2)
    ch[zh] = added([cz[i] for i in range(8)])
    c3 = send([(ch.at[zh], ch.at[zh], zp(d)) for d in (2, 1, 3)], ch.at[pl.ds(0, 3)])
    gathered(1, up, up_s)
    arrive(f_up)
    gr[up, x, y, one] = gr[up, x, y, one] + z1a[...]
    l_up = send([(gr.at[up, x, y], z2.at[0], zp(1))], z2.at[0])
    gathered(2, down, down_s)
    arrive(f_down)
    gr[down, x, y, two] = gr[down, x, y, two] + z1b[...]
    l_down = send([(gr.at[down, x, y], z2.at[1], zp(3))], z2.at[1])
    own_s = scatter2(3, zh, own_s)

    arrive(p2)
    ga_out[...] = psum[zl] + pz[0] + pz[1] + pz[2]
    stores = [
        pltpu.make_async_copy(src, dst, lsem.at[k])
        for k, (src, dst) in enumerate([(ga_out, ga_res), (gbt_out, gbt_res), (gc_out, gc_res)])
    ]
    stores[0].start()
    gathered(3, zh, own_s)

    arrive(l_up, l_down)
    got = gr[zh, x, y] + z2[0] + z2[1]
    gram_a = jnp.concatenate([got[4, :4], got[4, 4:]], 1)
    gram_c = jnp.concatenate([gcm[pl.ds(row * 4 + q, 1), :] for q in range(4)], 0)
    h = jnp.concatenate([gram_a * gram_c, jnp.zeros((12, 256), F32)], 0)
    h = dot3(split(h), (thi[1024:1280], tlo[1024:1280]), NN)[:4]
    for t in range(4):
        two = [h[:, (2 * t + i) * 128 : (2 * t + i + 1) * 128] for i in range(2)]
        gbt_out[t] = jnp.concatenate(two, 0) - got[t]
    stores[1].start()
    arrive(c3)
    gc_out[...] = added([ch[i] for i in range(4)])
    stores[2].start()
    for k, sized in enumerate(groups):
        pltpu.make_async_copy(sized, sized, ssem.at[k]).wait()
    for store in stores:
        store.wait()


def last(a_in, b_in, c_in, a_out, b_out, c_out):
    a_out[...] = a_in[...]
    b_out[...] = b_in[...]
    c_out[...] = c_in[...]


def local(tensor, factor_a, factor_bt, factor_c):
    bt = factor_bt.reshape(4, 8, 128).transpose(1, 0, 2).reshape(2, 16, 128)
    shapes = (
        jax.ShapeDtypeStruct((16, 256), F32),
        jax.ShapeDtypeStruct((4, 8, 128), F32),
        jax.ShapeDtypeStruct((8, 256), F32),
    )
    vmem = pl.BlockSpec(memory_space=pltpu.VMEM)
    parts = pl.pallas_call(
        kernel,
        out_shape=tuple(pltpu.VMEM(v.shape, v.dtype) for v in shapes),
        in_specs=[pl.BlockSpec(memory_space=pltpu.HBM)] * 4,
        out_specs=(pl.BlockSpec(memory_space=pl.ANY),) * 3,
        scratch_shapes=[
            pltpu.VMEM((8, 128, 1024), F32),
            pltpu.VMEM((1280, 1024), BF16),
            pltpu.VMEM((1280, 1024), BF16),
            pltpu.VMEM((256, 1024), BF16),
            pltpu.VMEM((256, 1024), BF16),
            pltpu.VMEM((4, 2, 16, 256), F32),
            pltpu.VMEM((4, 4, 4, 2, 16, 128), F32),
            pltpu.VMEM((8, 256, 128), F32),
            pltpu.VMEM((256, 256), F32),
            pltpu.VMEM((256, 256), F32),
            pltpu.VMEM((256, 256), F32),
            pltpu.VMEM((4, 4, 4, 5, 8, 128), F32),
            pltpu.VMEM((4, 3, 4, 2, 8, 128), F32),
            pltpu.VMEM((4, 3, 4, 3, 8, 128), F32),
            pltpu.VMEM((4, 3, 2, 8, 128), F32),
            pltpu.VMEM((4, 3, 3, 8, 128), F32),
            pltpu.VMEM((2, 8, 128), F32),
            pltpu.VMEM((3, 8, 128), F32),
            pltpu.VMEM((2, 5, 8, 128), F32),
            pltpu.VMEM((4, 2, 16, 256), F32),
            pltpu.VMEM((4, 16, 256), F32),
            pltpu.VMEM((4, 16, 256), F32),
            pltpu.VMEM((3, 16, 256), F32),
            pltpu.VMEM((8, 256), F32),
            pltpu.VMEM((16, 8, 256), F32),
            pltpu.VMEM((8, 8, 256), F32),
            pltpu.VMEM((4, 8, 256), F32),
            pltpu.VMEM((8, 256), F32),
            pltpu.VMEM((256, 128), F32),
            pltpu.VMEM((256, 128), F32),
            pltpu.VMEM((16, 256), F32),
            pltpu.VMEM((4, 8, 128), F32),
            pltpu.VMEM((8, 256), F32),
            pltpu.SemaphoreType.DMA((NSEM,)),
            pltpu.SemaphoreType.DMA((NSEM,)),
            pltpu.SemaphoreType.DMA((4,)),
        ],
        compiler_params=pltpu.CompilerParams(collective_id=0, has_side_effects=True),
    )(tensor, factor_a, bt, factor_c)
    grad_a, grad_bt, grad_c = pl.pallas_call(
        last, out_shape=shapes, in_specs=[vmem] * 3, out_specs=(vmem,) * 3
    )(*(pltpu.with_memory_space_constraint(v, pltpu.VMEM) for v in parts))
    grad_bt = grad_bt.reshape(8, 4, 128).transpose(1, 0, 2).reshape(4, 1024)
    return grad_a, grad_bt, grad_c


def solution(mesh):
    in_specs = (P(None, "row", "col"), P(("row", "col"), None), P("row", "col"), P())
    out_specs = (P(("row", "col"), None), P("row", "col"), P())
    return jax.shard_map(local, mesh=mesh, in_specs=in_specs, out_specs=out_specs, check_vma=False)
```
